256 devices in a mesh: gx: 16 (over z, core), yz: 16 (over y, x).
Axes of the slice: x: 4, y: 4, z: 8, core: 2. Of those that a mesh axis runs over, the one named last changes fastest.
Arguments:
- state: float32 [5, 256, 256, 256], P(None, 'gx', 'yz'), may hold values from -3 to 9, as said below
- register: float32 [5, 256, 256, 256], P(None, 'gx', 'yz'), may hold values from -4 to 4
Outputs:
- register_out: float32 [5, 256, 256, 256], P(None, 'gx', 'yz')
- filtered: float32 [5, 256, 256, 256], P(None, 'gx', 'yz')
The draws below stay inside these ranges and needn't reach their ends.
Inputs may be any that keep to these rules, and one draw needn't show every extreme that they name: state holds the density, the three momenta and the total energy of an ideal gas with ratio of specific heats 1.4; in every cell the density lies between 0.4 and 2.2 and the pressure between 0.4 and 2.1.
All inputs are finite; a program needn't handle non-finite values.
Results may differ from the reference program's by a relative error of at most 0.0003.
Values sent between devices are 32-bit elements; how exact they have to be, the bound alone decides.
No kernel may reach another device: no remote copies, remote signals or barrier semaphores. Data moves between devices by JAX's collectives and lax.ppermute only.
A program may use at most 128 MiB of HBM per device.

```python
import jax
import jax.numpy as jnp

NZ = 256
NX = 256
NY = 256


def draw_state(key, part):
    keys = jax.random.split(key, 3)
    shape = (NX, NY, NZ)
    coord_x = (2.0 * jnp.pi / NX * jnp.arange(NX, dtype=jnp.float32))[:, None, None]
    coord_y = (2.0 * jnp.pi / NY * jnp.arange(NY, dtype=jnp.float32))[None, :, None]
    coord_z = (2.0 * jnp.pi / NZ * jnp.arange(NZ, dtype=jnp.float32))[None, None, :]
    waves = jnp.cos(2.0 * coord_x) + jnp.cos(2.0 * coord_y)
    density = jnp.exp(jax.random.uniform(keys[0], shape, jnp.float32, -0.5, 0.5))
    rough = 0.25 * jax.random.truncated_normal(keys[1], -3.0, 3.0, (3,) + shape, jnp.float32)
    swirl = 0.5
    pressure = jnp.exp(jax.random.uniform(keys[2], shape, jnp.float32, -0.5, 0.5)) * (1.0 + 0.1 * waves)
    speed_x = swirl * jnp.sin(coord_x) * jnp.cos(coord_y) * jnp.cos(coord_z) + rough[0]
    speed_y = -swirl * jnp.cos(coord_x) * jnp.sin(coord_y) * jnp.cos(coord_z) + rough[1]
    speed_z = rough[2]
    energy = pressure / 0.4 + 0.5 * density * (speed_x * speed_x + speed_y * speed_y + speed_z * speed_z)
    return jnp.stack([density, density * speed_x, density * speed_y, density * speed_z, energy]).astype(jnp.float32)


def level_of(own_key, dims, pieces, least, largest):
    loudness, own = 1.0, jax.random.fold_in(own_key, 6)
    for position, shards_of in pieces:
        steps = jnp.exp(jax.random.uniform(jax.random.fold_in(own, position), (shards_of,), jnp.float32, least / len(pieces), largest / len(pieces)))
        loudness = loudness * jnp.repeat(steps, dims[position] // shards_of).reshape([-1 if axis == position else 1 for axis in range(len(dims))])
    return loudness


def noise(key, dims, spread, limit, cuts=(), kind=jnp.bfloat16):
    entries = spread * jax.random.normal(key, dims, jnp.float32)
    if cuts:
        entries = entries * level_of(key, dims, cuts, -0.22, 0.18)
    return jnp.clip(entries, -limit, limit).astype(kind)


def setup_inputs(seed: int = 0) -> dict:
    streams_of = jax.random.split(jax.random.key(seed), 3)
    return {
        "state": draw_state(jax.random.fold_in(streams_of[2], 71), 0),
        "register": noise(streams_of[1], (5, NX, NY, NZ), 0.3, 4.0, ((1, 16), (2, 16)), jnp.float32),
    }


gamma_gas = 1.4
central_weights = (4.0 / 5.0, -1.0 / 5.0, 4.0 / 105.0, -1.0 / 280.0)
filter_alpha = 0.49
register_decay = -5.0 / 9.0
register_gain = 15.0 / 16.0
time_step = 0.2


def primitives(fields):
    density = fields[0]
    speed_x = fields[1] / density
    speed_y = fields[2] / density
    speed_z = fields[3] / density
    kinetic = 0.5 * density * (speed_x * speed_x + speed_y * speed_y + speed_z * speed_z)
    pressure = (gamma_gas - 1.0) * (fields[4] - kinetic)
    enthalpy = (fields[4] + pressure) / density
    return (density, speed_x, speed_y, speed_z, pressure, enthalpy)


def pair_flux(left, right, direction):
    means = [0.5 * (one + other) for one, other in zip(left, right)]
    density, speed_x, speed_y, speed_z, pressure, enthalpy = means
    normal = (speed_x, speed_y, speed_z)[direction]
    mass = density * normal
    moment = [mass * speed_x, mass * speed_y, mass * speed_z]
    moment[direction] = moment[direction] + pressure
    return [mass] + moment + [mass * enthalpy]


def residual_of(state):
    prims = primitives(state)
    total = [jnp.zeros_like(state[0]) for field in range(5)]
    for direction in range(3):
        for offset in range(1, 5):
            weight = central_weights[offset - 1]
            ahead = tuple(jnp.roll(column, -offset, axis=direction) for column in prims)
            flux = pair_flux(prims, ahead, direction)
            total = [part - 2.0 * weight * (value - jnp.roll(value, offset, axis=direction)) for part, value in zip(total, flux)]
    return jnp.stack(total)


def reference(state, register):
    residual = residual_of(state)
    register_out = register_decay * register + time_step * residual
    section = state + register_gain * register_out
    alpha = filter_alpha
    coeffs = ((11.0 + 10.0 * alpha) / 16.0, (15.0 + 34.0 * alpha) / 32.0, (-3.0 + 6.0 * alpha) / 16.0, (1.0 - 2.0 * alpha) / 32.0)
    rhs = coeffs[0] * section
    for shift in range(1, 4):
        rhs = rhs + (coeffs[shift] / 2.0) * (jnp.roll(section, -shift, axis=1) + jnp.roll(section, shift, axis=1))
    waves = jnp.arange(NX // 2 + 1, dtype=jnp.float32)
    eigen = 1.0 + 2.0 * alpha * jnp.cos((2.0 * jnp.pi / NX) * waves)
    spectrum = jnp.fft.rfft(rhs, axis=1)
    filtered = jnp.fft.irfft(spectrum / eigen[None, :, None, None], n=NX, axis=1)
    return register_out, filtered.astype(jnp.float32)
```

```python
import math

import jax
import jax.numpy as jnp
from jax import lax
from jax.experimental import pallas as pl
from jax.experimental.pallas import tpu as pltpu
from jax.sharding import PartitionSpec as P

gamma_gas = 1.4
central_weights = (4.0 / 5.0, -1.0 / 5.0, 4.0 / 105.0, -1.0 / 280.0)
filter_alpha = 0.49
register_decay = -5.0 / 9.0
register_gain = 15.0 / 16.0
time_step = 0.2

ROOT = (-1.0 + math.sqrt(1.0 - 4.0 * filter_alpha**2)) / (2.0 * filter_alpha)
GREEN = 1.0 / math.sqrt(1.0 - 4.0 * filter_alpha**2)
TAPS = (
    (11.0 + 10.0 * filter_alpha) / 16.0,
    (15.0 + 34.0 * filter_alpha) / 64.0,
    (-3.0 + 6.0 * filter_alpha) / 32.0,
    (1.0 - 2.0 * filter_alpha) / 64.0,
)
KAPPA = GREEN * sum(TAPS[abs(n)] * ROOT**n for n in range(-3, 4))
DELTA = tuple(
    GREEN * sum(TAPS[abs(n)] * ROOT ** abs(d - n) for n in range(-3, 4)) - KAPPA * ROOT**d
    for d in range(3)
)

VMEM = pl.BlockSpec(memory_space=pltpu.VMEM)
SMEM = pl.BlockSpec(memory_space=pltpu.SMEM)
F32 = jnp.float32


def primitives(fields):
    density, mom_x, mom_y, mom_z, energy = fields
    inverse = 1.0 / density
    speed_x, speed_y, speed_z = mom_x * inverse, mom_y * inverse, mom_z * inverse
    kinetic = 0.5 * (mom_x * speed_x + mom_y * speed_y + mom_z * speed_z)
    pressure = (gamma_gas - 1.0) * (energy - kinetic)
    return (density, speed_x, speed_y, speed_z, pressure, (energy + pressure) * inverse)


def pair_flux(left, right, direction, weight):
    density, speed_x, speed_y, speed_z, pressure, enthalpy = [a + b for a, b in zip(left, right)]
    normal = (speed_x, speed_y, speed_z)[direction]
    mass = (density * normal) * (0.25 * weight)
    moment = [mass * speed_x, mass * speed_y, mass * speed_z]
    moment[direction] = moment[direction] + pressure * weight
    return [mass + mass] + moment + [mass * enthalpy]


def rows_of(shape, dim):
    return lax.broadcasted_iota(jnp.int32, shape, dim)


def inner_kernel(state_ref, acc_ref, prim_ref):
    @pl.loop(0, 16)
    def _(x):
        for half in range(2):
            rows = pl.ds(8 * half, 8)
            for f, value in enumerate(primitives([state_ref[f, x, rows, :] for f in range(5)])):
                prim_ref[f, x, rows, :] = value

    @pl.loop(0, 16)
    def _(x):
        for half in range(2):
            rows = pl.ds(8 * half, 8)
            own = [prim_ref[f, x, rows, :] for f in range(6)]
            total = [jnp.zeros((8, 256), F32)] * 5
            for l in range(1, 5):
                ahead = [pltpu.roll(value, 256 - l, 1) for value in own]
                flux = pair_flux(own, ahead, 2, central_weights[l - 1])
                total = [part + (pltpu.roll(value, l, 1) - value) for part, value in zip(total, flux)]
            for f in range(5):
                acc_ref[f, x, rows, :] = total[f]

    row = rows_of((16, 128), 0)

    @pl.loop(0, 16)
    def _(x):
        for half in range(2):
            lanes = pl.ds(128 * half, 128)
            own = [prim_ref[f, x, :, lanes] for f in range(6)]
            total = [acc_ref[f, x, :, lanes] for f in range(5)]
            for l in range(1, 5):
                ahead = [pltpu.roll(value, 16 - l, 0) for value in own]
                weight = jnp.where(row < 16 - l, F32(central_weights[l - 1]), F32(0.0))
                flux = pair_flux(own, ahead, 1, weight)
                total = [part + (pltpu.roll(value, l, 0) - value) for part, value in zip(total, flux)]
            for f in range(5):
                acc_ref[f, x, :, lanes] = total[f]

    for half in range(2):
        lanes = pl.ds(128 * half, 128)

        @pl.loop(0, 2)
        def _(tile):
            rows = pl.ds(pl.multiple_of(8 * tile, 8), 8)
            for x in range(16):
                own = [prim_ref[f, x, rows, lanes] for f in range(6)]
                total = [acc_ref[f, x, rows, lanes] for f in range(5)]
                for l in range(1, min(5, 16 - x)):
                    ahead = [prim_ref[f, x + l, rows, lanes] for f in range(6)]
                    flux = pair_flux(own, ahead, 0, central_weights[l - 1])
                    for f in range(5):
                        total[f] = total[f] - flux[f]
                        acc_ref[f, x + l, rows, lanes] = acc_ref[f, x + l, rows, lanes] + flux[f]
                for f in range(5):
                    acc_ref[f, x, rows, lanes] = total[f]


def edge_kernel(
    even_ref, state_ref, register_ref, part_ref, xa_ref, xb_ref, ya_ref, yb_ref,
    out_ref, section_ref, moment_ref, acc_ref, prim_ref, far_ref,
):
    even = even_ref[0] == 1
    row = rows_of((8, 128), 0)

    @pl.loop(0, 16)
    def _(x):
        for half in range(2):
            lanes = pl.ds(128 * half, 128)
            left, right = [], []
            for f in range(5):
                a, b = ya_ref[f, x, :, lanes], yb_ref[f, x, :, lanes]
                below, above = jnp.where(even, a, b), jnp.where(even, b, a)
                left.append(jnp.concatenate([below, state_ref[f, x, 12:16, lanes]], axis=0))
                right.append(jnp.concatenate([state_ref[f, x, 0:4, lanes], above], axis=0))
            left, right = primitives(left), primitives(right)
            low = [jnp.zeros((8, 128), F32)] * 5
            high = [jnp.zeros((8, 128), F32)] * 5
            for l in range(1, 5):
                weight = jnp.where(lax.rem(row, 4) >= 4 - l, F32(central_weights[l - 1]), F32(0.0))
                other = right if l == 4 else [pltpu.roll(value, 4 - l, 0) for value in right]
                flux = pair_flux(left, other, 1, weight)
                high = [part - value for part, value in zip(high, flux)]
                back = flux if l == 4 else [pltpu.roll(value, 4 + l, 0) for value in flux]
                low = [part + value for part, value in zip(low, back)]
            for f in range(5):
                acc_ref[f, x, 0:8, lanes] = part_ref[f, x, 0:8, lanes] + jnp.where(row < 4, low[f], 0.0)
                acc_ref[f, x, 8:16, lanes] = part_ref[f, x, 8:16, lanes] + jnp.where(row >= 4, high[f], 0.0)

    @pl.loop(0, 4)
    def _(x):
        for tile in range(2):
            rows = pl.ds(8 * tile, 8)
            a = [xa_ref[f, x, rows, :] for f in range(5)]
            b = [xb_ref[f, x, rows, :] for f in range(5)]
            before = primitives([jnp.where(even, v, u) for u, v in zip(a, b)])
            after = primitives([jnp.where(even, u, v) for u, v in zip(a, b)])
            first = primitives([state_ref[f, x, rows, :] for f in range(5)])
            last = primitives([state_ref[f, x + 12, rows, :] for f in range(5)])
            for f in range(6):
                far_ref[0, f, x, rows, :] = before[f]
                far_ref[1, f, x, rows, :] = after[f]
                prim_ref[0, f, x, rows, :] = first[f]
                prim_ref[1, f, x, rows, :] = last[f]

    for half in range(2):
        lanes = pl.ds(128 * half, 128)

        @pl.loop(0, 2)
        def _(tile):
            rows = pl.ds(pl.multiple_of(8 * tile, 8), 8)
            for x in range(4):
                own = [prim_ref[0, f, x, rows, lanes] for f in range(6)]
                total = [acc_ref[f, x, rows, lanes] for f in range(5)]
                for l in range(x + 1, 5):
                    left = [far_ref[0, f, 4 + x - l, rows, lanes] for f in range(6)]
                    flux = pair_flux(left, own, 0, central_weights[l - 1])
                    total = [part + value for part, value in zip(total, flux)]
                for f in range(5):
                    acc_ref[f, x, rows, lanes] = total[f]
            for x in range(4):
                own = [prim_ref[1, f, x, rows, lanes] for f in range(6)]
                total = [acc_ref[f, x + 12, rows, lanes] for f in range(5)]
                for l in range(4 - x, 5):
                    right = [far_ref[1, f, x + l - 4, rows, lanes] for f in range(6)]
                    flux = pair_flux(own, right, 0, central_weights[l - 1])
                    total = [part - value for part, value in zip(total, flux)]
                for f in range(5):
                    acc_ref[f, x + 12, rows, lanes] = total[f]

    @pl.loop(0, 5)
    def _(f):
        for tile in range(2):
            rows = pl.ds(8 * tile, 8)
            forward = jnp.zeros((8, 256), F32)
            backward = jnp.zeros((8, 256), F32)
            for x in range(16):
                value = register_decay * register_ref[f, x, rows, :] + time_step * acc_ref[f, x, rows, :]
                out_ref[f, x, rows, :] = value
                value = state_ref[f, x, rows, :] + register_gain * value
                section_ref[f, x, rows, :] = value
                forward = value + ROOT * forward
                backward = backward + ROOT**x * value
            for pair in range(4):
                for half in range(2):
                    q = 2 * (4 * tile + pair) + half
                    lanes = slice(128 * half, 128 * half + 128)
                    moment_ref[q, 0, f] = forward[2 * pair : 2 * pair + 2, lanes]
                    moment_ref[q, 1, f] = backward[2 * pair : 2 * pair + 2, lanes]


def ring_kernel(moment_ref, sums_ref):
    decay = ROOT**16
    close = 1.0 / (1.0 - ROOT**256)
    for f in range(5):
        value = jnp.zeros((2, 128), F32)
        for p in range(16):
            value = moment_ref[p, 0, f] + decay * value
        value = value * close
        for p in range(16):
            sums_ref[p, 0, f] = value
            value = moment_ref[p, 0, f] + decay * value
        value = jnp.zeros((2, 128), F32)
        for p in reversed(range(16)):
            value = moment_ref[p, 1, f] + decay * value
        value = value * close
        for p in reversed(range(16)):
            sums_ref[p, 1, f] = value
            value = moment_ref[p, 1, f] + decay * value


def filter_kernel(even_ref, section_ref, sums_ref, xa_ref, xb_ref, out_ref, ends_ref):
    even = even_ref[0] == 1
    for q in range(16):
        rows = pl.ds(2 * (q // 2), 2)
        lanes = pl.ds(128 * (q % 2), 128)
        for f in range(5):
            ends_ref[0, f, rows, lanes] = sums_ref[q, 0, f]
            ends_ref[1, f, rows, lanes] = sums_ref[q, 1, f]

    @pl.loop(0, 5)
    def _(f):
        for tile in range(2):
            for half in range(2):
                rows, lanes = pl.ds(8 * tile, 8), pl.ds(128 * half, 128)
                a = [xa_ref[f, k, rows, lanes] for k in range(2)]
                b = [xb_ref[f, k, rows, lanes] for k in range(2)]
                cells = [jnp.where(even, v, u) for u, v in zip(a, b)]
                cells += [section_ref[f, x, rows, lanes] for x in range(16)]
                cells += [jnp.where(even, u, v) for u, v in zip(a, b)]
                value = ends_ref[0, f, rows, lanes]
                forward = []
                for x in range(16):
                    value = cells[x + 2] + ROOT * value
                    forward.append(value)
                value = ends_ref[1, f, rows, lanes]
                for x in reversed(range(16)):
                    value = cells[x + 2] + ROOT * value
                    out_ref[f, x, rows, lanes] = (
                        KAPPA * (forward[x] + value)
                        + (DELTA[0] - KAPPA) * cells[x + 2]
                        + DELTA[1] * (cells[x + 1] + cells[x + 3])
                        + DELTA[2] * (cells[x] + cells[x + 4])
                    )


def permutation(step_x, step_y):
    pairs = []
    for g in range(16):
        sign = 1 if g % 2 == 0 else -1
        for y in range(16):
            target = (g + sign * step_x) % 16 * 16 + (y + sign * step_y) % 16
            pairs.append((g * 16 + y, target))
    return pairs


def body(state, register):
    axes = ("gx", "yz")
    shape = (5, 16, 16, 256)
    even = lax.rem(lax.axis_index("gx"), 2) == 0
    even_flag = jnp.reshape(even.astype(jnp.int32), (1,))
    block = jax.ShapeDtypeStruct(shape, F32)
    lines = jax.ShapeDtypeStruct((16, 2, 5, 2, 128), F32)

    y_high, y_low = state[:, :, 12:16], state[:, :, 0:4]
    x_high, x_low = state[:, 12:16], state[:, 0:4]
    ya = lax.ppermute(jnp.where(even, y_high, y_low), axes, permutation(0, 1))
    yb = lax.ppermute(jnp.where(even, y_low, y_high), axes, permutation(0, -1))
    xa = lax.ppermute(jnp.where(even, x_high, x_low), axes, permutation(1, 0))
    xb = lax.ppermute(jnp.where(even, x_low, x_high), axes, permutation(-1, 0))

    part = pl.pallas_call(
        inner_kernel,
        out_shape=block,
        in_specs=[VMEM],
        out_specs=VMEM,
        scratch_shapes=[pltpu.VMEM((6, 16, 16, 256), F32)],
        name="inner",
    )(state)

    register_out, section, moments = pl.pallas_call(
        edge_kernel,
        out_shape=(block, block, lines),
        in_specs=[SMEM] + [VMEM] * 7,
        out_specs=(VMEM, VMEM, VMEM),
        scratch_shapes=[
            pltpu.VMEM(shape, F32),
            pltpu.VMEM((2, 6, 4, 16, 256), F32),
            pltpu.VMEM((2, 6, 4, 16, 256), F32),
        ],
        name="edge",
    )(even_flag, state, register, part, xa, xb, ya, yb)

    s_high, s_low = section[:, 14:16], section[:, 0:2]
    sa = lax.ppermute(jnp.where(even, s_high, s_low), axes, permutation(1, 0))
    sb = lax.ppermute(jnp.where(even, s_low, s_high), axes, permutation(-1, 0))

    moments = lax.all_to_all(moments, "gx", 0, 0, tiled=True)
    sums = pl.pallas_call(
        ring_kernel, out_shape=lines, in_specs=[VMEM], out_specs=VMEM, name="ring"
    )(moments)
    sums = lax.all_to_all(sums, "gx", 0, 0, tiled=True)

    filtered = pl.pallas_call(
        filter_kernel,
        out_shape=block,
        in_specs=[SMEM] + [VMEM] * 4,
        out_specs=VMEM,
        scratch_shapes=[pltpu.VMEM((2, 5, 16, 256), F32)],
        name="filter",
    )(even_flag, section, sums, sa, sb)
    return (register_out, filtered)


def solution(mesh):
    spec = P(None, "gx", "yz", None)
    return jax.shard_map(
        body, mesh=mesh, in_specs=(spec, spec), out_specs=(spec, spec), check_vma=False
    )
```

```python
import math

import jax
import jax.numpy as jnp
from jax import lax
from jax.experimental import pallas as pl
from jax.experimental.pallas import tpu as pltpu
from jax.sharding import PartitionSpec as P

gamma_gas = 1.4
central_weights = (4.0 / 5.0, -1.0 / 5.0, 4.0 / 105.0, -1.0 / 280.0)
filter_alpha = 0.49
register_decay = -5.0 / 9.0
register_gain = 15.0 / 16.0
time_step = 0.2

ROOT = (-1.0 + math.sqrt(1.0 - 4.0 * filter_alpha**2)) / (2.0 * filter_alpha)
GREEN = 1.0 / math.sqrt(1.0 - 4.0 * filter_alpha**2)
TAPS = (
    (11.0 + 10.0 * filter_alpha) / 16.0,
    (15.0 + 34.0 * filter_alpha) / 64.0,
    (-3.0 + 6.0 * filter_alpha) / 32.0,
    (1.0 - 2.0 * filter_alpha) / 64.0,
)
KAPPA = GREEN * sum(TAPS[abs(n)] * ROOT**n for n in range(-3, 4))
DELTA = tuple(
    GREEN * sum(TAPS[abs(n)] * ROOT ** abs(d - n) for n in range(-3, 4)) - KAPPA * ROOT**d
    for d in range(3)
)

VMEM = pl.BlockSpec(memory_space=pltpu.VMEM)
SMEM = pl.BlockSpec(memory_space=pltpu.SMEM)
ANY = pl.BlockSpec(memory_space=pl.ANY)
F32 = jnp.float32
GRANT = pltpu.CompilerParams(vmem_limit_bytes=16 << 20)


def near(value):
    return pltpu.with_memory_space_constraint(value, pltpu.VMEM)


def primitives(fields):
    density, mom_x, mom_y, mom_z, energy = fields
    inverse = 1.0 / density
    speed_x, speed_y, speed_z = mom_x * inverse, mom_y * inverse, mom_z * inverse
    kinetic = 0.5 * (mom_x * speed_x + mom_y * speed_y + mom_z * speed_z)
    pressure = (gamma_gas - 1.0) * (energy - kinetic)
    return (density, speed_x, speed_y, speed_z, pressure, (energy + pressure) * inverse)


def pair_flux(left, right, direction, weight):
    density, speed_x, speed_y, speed_z, pressure, enthalpy = [a + b for a, b in zip(left, right)]
    normal = (speed_x, speed_y, speed_z)[direction]
    mass = (density * normal) * (0.25 * weight)
    moment = [mass * speed_x, mass * speed_y, mass * speed_z]
    moment[direction] = moment[direction] + pressure * weight
    return [mass + mass] + moment + [mass * enthalpy]


def rows_of(shape, dim):
    return lax.broadcasted_iota(jnp.int32, shape, dim)


def pack_kernel(even_ref, state_any, state_ref, ya_ref, yb_ref, xa_ref, xb_ref, sems):
    copies = [pltpu.make_async_copy(state_any.at[f], state_ref.at[f], sems.at[f]) for f in range(5)]
    for copy in copies:
        copy.start()
    even = even_ref[0] == 1
    for f in range(5):
        copies[f].wait()

        @pl.loop(0, 4)
        def _(step):
            for k in range(4):
                x = 4 * step + k
                low, high = state_ref[f, x, 0:4, :], state_ref[f, x, 12:16, :]
                ya_ref[f, x] = jnp.where(even, high, low)
                yb_ref[f, x] = jnp.where(even, low, high)
            xa_ref[f, step] = state_ref[f, jnp.where(even, 12, 0) + step]
            xb_ref[f, step] = state_ref[f, jnp.where(even, 0, 12) + step]


def inner_kernel(state_ref, part_ref, prim_ref):
    row = rows_of((16, 128), 0)
    below = [jnp.where(row < 16 - l, F32(central_weights[l - 1]), F32(0.0)) for l in range(1, 5)]

    @pl.loop(0, 16)
    def _(x):
        prims = [primitives([state_ref[f, x, 8 * half : 8 * half + 8, :] for f in range(5)]) for half in range(2)]
        along = [[None, None] for _ in range(5)]
        for half in range(2):
            own = prims[half]
            for f in range(6):
                prim_ref[f, x, 8 * half : 8 * half + 8, :] = own[f]
            total = [jnp.zeros((8, 256), F32)] * 5
            for l in range(1, 5):
                ahead = [pltpu.roll(value, 256 - l, 1) for value in own]
                flux = pair_flux(own, ahead, 2, central_weights[l - 1])
                total = [part + (pltpu.roll(value, l, 1) - value) for part, value in zip(total, flux)]
            for f in range(5):
                along[f][half] = total[f]
        for half in range(2):
            lanes = pl.ds(128 * half, 128)
            cut = slice(128 * half, 128 * half + 128)
            own = [jnp.concatenate([prims[0][f][:, cut], prims[1][f][:, cut]], axis=0) for f in range(6)]
            total = [jnp.zeros((16, 128), F32)] * 5
            for l in range(1, 5):
                ahead = [pltpu.roll(value, 16 - l, 0) for value in own]
                flux = pair_flux(own, ahead, 1, below[l - 1])
                total = [part + (pltpu.roll(value, l, 0) - value) for part, value in zip(total, flux)]
            for f in range(5):
                part_ref[f, x, :, lanes] = total[f] + jnp.concatenate(
                    [along[f][0][:, cut], along[f][1][:, cut]], axis=0
                )

    for half in range(2):
        lanes = pl.ds(128 * half, 128)

        @pl.loop(0, 2)
        def _(tile):
            rows = pl.ds(pl.multiple_of(8 * tile, 8), 8)
            for x in range(16):
                own = [prim_ref[f, x, rows, lanes] for f in range(6)]
                total = [part_ref[f, x, rows, lanes] for f in range(5)]
                for l in range(1, min(5, 16 - x)):
                    ahead = [prim_ref[f, x + l, rows, lanes] for f in range(6)]
                    flux = pair_flux(own, ahead, 0, central_weights[l - 1])
                    for f in range(5):
                        total[f] = total[f] - flux[f]
                        part_ref[f, x + l, rows, lanes] = part_ref[f, x + l, rows, lanes] + flux[f]
                for f in range(5):
                    part_ref[f, x, rows, lanes] = total[f]


def edge_kernel(
    even_ref, state_ref, part_ref, register_any, xa_any, xb_any, ya_any, yb_any,
    out_any, section_any, moment_ref, sa_ref, sb_ref,
    acc_ref, prim_ref, far_ref, register_ref, xa_ref, xb_ref, ya_ref, yb_ref, out_ref, section_ref,
    in_sems, out_sems,
):
    even = even_ref[0] == 1
    row = rows_of((8, 128), 0)
    arrivals = [
        pltpu.make_async_copy(source, target, in_sems.at[k])
        for k, (source, target) in enumerate(
            ((xa_any, xa_ref), (xb_any, xb_ref), (ya_any, ya_ref), (yb_any, yb_ref), (register_any, register_ref))
        )
    ]
    for copy in arrivals:
        copy.start()
    departures = [
        [
            pltpu.make_async_copy(out_ref.at[f], out_any.at[f], out_sems.at[0, f]),
            pltpu.make_async_copy(section_ref.at[f], section_any.at[f], out_sems.at[1, f]),
        ]
        for f in range(5)
    ]

    @pl.loop(4, 12)
    def _(x):
        for f in range(5):
            acc_ref[f, x] = part_ref[f, x]

    @pl.loop(0, 4)
    def _(x):
        for tile in range(2):
            rows = pl.ds(8 * tile, 8)
            first = primitives([state_ref[f, x, rows, :] for f in range(5)])
            last = primitives([state_ref[f, x + 12, rows, :] for f in range(5)])
            for f in range(6):
                prim_ref[0, f, x, rows, :] = first[f]
                prim_ref[1, f, x, rows, :] = last[f]

    arrivals[0].wait()
    arrivals[1].wait()

    @pl.loop(0, 4)
    def _(x):
        for tile in range(2):
            rows = pl.ds(8 * tile, 8)
            a = [xa_ref[f, x, rows, :] for f in range(5)]
            b = [xb_ref[f, x, rows, :] for f in range(5)]
            before = primitives([jnp.where(even, v, u) for u, v in zip(a, b)])
            after = primitives([jnp.where(even, u, v) for u, v in zip(a, b)])
            for f in range(6):
                far_ref[0, f, x, rows, :] = before[f]
                far_ref[1, f, x, rows, :] = after[f]

    for half in range(2):
        lanes = pl.ds(128 * half, 128)

        @pl.loop(0, 2)
        def _(tile):
            rows = pl.ds(pl.multiple_of(8 * tile, 8), 8)
            for x in range(4):
                own = [prim_ref[0, f, x, rows, lanes] for f in range(6)]
                total = [part_ref[f, x, rows, lanes] for f in range(5)]
                for l in range(x + 1, 5):
                    left = [far_ref[0, f, 4 + x - l, rows, lanes] for f in range(6)]
                    flux = pair_flux(left, own, 0, central_weights[l - 1])
                    total = [part + value for part, value in zip(total, flux)]
                for f in range(5):
                    acc_ref[f, x, rows, lanes] = total[f]
            for x in range(4):
                own = [prim_ref[1, f, x, rows, lanes] for f in range(6)]
                total = [part_ref[f, x + 12, rows, lanes] for f in range(5)]
                for l in range(4 - x, 5):
                    right = [far_ref[1, f, x + l - 4, rows, lanes] for f in range(6)]
                    flux = pair_flux(own, right, 0, central_weights[l - 1])
                    total = [part - value for part, value in zip(total, flux)]
                for f in range(5):
                    acc_ref[f, x + 12, rows, lanes] = total[f]

    arrivals[2].wait()
    arrivals[3].wait()

    @pl.loop(0, 16)
    def _(x):
        for half in range(2):
            lanes = pl.ds(128 * half, 128)
            left, right = [], []
            for f in range(5):
                a, b = ya_ref[f, x, :, lanes], yb_ref[f, x, :, lanes]
                below, above = jnp.where(even, a, b), jnp.where(even, b, a)
                left.append(jnp.concatenate([below, state_ref[f, x, 12:16, lanes]], axis=0))
                right.append(jnp.concatenate([state_ref[f, x, 0:4, lanes], above], axis=0))
            left, right = primitives(left), primitives(right)
            low = [jnp.zeros((8, 128), F32)] * 5
            high = [jnp.zeros((8, 128), F32)] * 5
            for l in range(1, 5):
                weight = jnp.where(lax.rem(row, 4) >= 4 - l, F32(central_weights[l - 1]), F32(0.0))
                other = right if l == 4 else [pltpu.roll(value, 4 - l, 0) for value in right]
                flux = pair_flux(left, other, 1, weight)
                high = [part - value for part, value in zip(high, flux)]
                back = flux if l == 4 else [pltpu.roll(value, 4 + l, 0) for value in flux]
                low = [part + value for part, value in zip(low, back)]
            for f in range(5):
                acc_ref[f, x, 0:8, lanes] = acc_ref[f, x, 0:8, lanes] + jnp.where(row < 4, low[f], 0.0)
                acc_ref[f, x, 8:16, lanes] = acc_ref[f, x, 8:16, lanes] + jnp.where(row >= 4, high[f], 0.0)

    arrivals[4].wait()
    for f in range(5):

        @pl.loop(0, 2)
        def _(tile):
            rows = pl.ds(pl.multiple_of(8 * tile, 8), 8)
            forward = jnp.zeros((8, 256), F32)
            backward = jnp.zeros((8, 256), F32)
            for x in range(16):
                value = register_decay * register_ref[f, x, rows, :] + time_step * acc_ref[f, x, rows, :]
                out_ref[f, x, rows, :] = value
                value = state_ref[f, x, rows, :] + register_gain * value
                section_ref[f, x, rows, :] = value
                forward = value + ROOT * forward
                backward = backward + ROOT**x * value
            for pair in range(4):
                for half in range(2):
                    q = 2 * (4 * tile + pair) + half
                    lanes = slice(128 * half, 128 * half + 128)
                    moment_ref[q, 0, f] = forward[2 * pair : 2 * pair + 2, lanes]
                    moment_ref[q, 1, f] = backward[2 * pair : 2 * pair + 2, lanes]
        for copy in departures[f]:
            copy.start()
        for k in range(2):
            sa_ref[f, k] = section_ref[f, jnp.where(even, 14, 0) + k]
            sb_ref[f, k] = section_ref[f, jnp.where(even, 0, 14) + k]
    for pair in departures:
        for copy in pair:
            copy.wait()


def ring_kernel(moment_ref, local_any, sums_ref):
    decay = ROOT**16
    close = 1.0 / (1.0 - ROOT**256)
    for f in range(5):
        value = jnp.zeros((2, 128), F32)
        for p in range(16):
            value = moment_ref[p, 0, f] + decay * value
        value = value * close
        for p in range(16):
            sums_ref[p, 0, f] = value
            value = moment_ref[p, 0, f] + decay * value
        value = jnp.zeros((2, 128), F32)
        for p in reversed(range(16)):
            value = moment_ref[p, 1, f] + decay * value
        value = value * close
        for p in reversed(range(16)):
            sums_ref[p, 1, f] = value
            value = moment_ref[p, 1, f] + decay * value


def local_kernel(even_ref, section_any, xa_ref, xb_ref, out_ref, section_ref, sems):
    even = even_ref[0] == 1
    arrivals = [pltpu.make_async_copy(section_any.at[f], section_ref.at[f], sems.at[f]) for f in range(5)]
    for copy in arrivals:
        copy.start()
    for f in range(5):
        arrivals[f].wait()

        @pl.loop(0, 2)
        def _(tile):
            for half in range(2):
                rows, lanes = pl.ds(pl.multiple_of(8 * tile, 8), 8), pl.ds(128 * half, 128)
                a = [xa_ref[f, k, rows, lanes] for k in range(2)]
                b = [xb_ref[f, k, rows, lanes] for k in range(2)]
                cells = [jnp.where(even, v, u) for u, v in zip(a, b)]
                cells += [section_ref[f, x, rows, lanes] for x in range(16)]
                cells += [jnp.where(even, u, v) for u, v in zip(a, b)]
                value = cells[2]
                forward = [value]
                for x in range(1, 16):
                    value = cells[x + 2] + ROOT * value
                    forward.append(value)
                value = jnp.zeros((8, 128), F32)
                for x in reversed(range(16)):
                    value = cells[x + 2] + ROOT * value
                    out_ref[f, x, rows, lanes] = (
                        KAPPA * (forward[x] + value)
                        + (DELTA[0] - KAPPA) * cells[x + 2]
                        + DELTA[1] * (cells[x + 1] + cells[x + 3])
                        + DELTA[2] * (cells[x] + cells[x + 4])
                    )


def filter_kernel(local_ref, sums_ref, out_ref, ends_ref, full_ref, sems):
    for q in range(16):
        rows = pl.ds(2 * (q // 2), 2)
        lanes = pl.ds(128 * (q % 2), 128)
        for f in range(5):
            ends_ref[0, f, rows, lanes] = sums_ref[q, 0, f]
            ends_ref[1, f, rows, lanes] = sums_ref[q, 1, f]
    copies = [pltpu.make_async_copy(full_ref.at[f], out_ref.at[f], sems.at[f]) for f in range(5)]
    for f in range(5):

        @pl.loop(0, 2)
        def _(tile):
            rows = pl.ds(pl.multiple_of(8 * tile, 8), 8)
            before, after = ends_ref[0, f, rows, :], ends_ref[1, f, rows, :]
            for x in range(16):
                full_ref[f, x, rows, :] = local_ref[f, x, rows, :] + (
                    KAPPA * ROOT ** (x + 1) * before + KAPPA * ROOT ** (16 - x) * after
                )

        copies[f].start()
    for copy in copies:
        copy.wait()


def permutation(step_x, step_y):
    pairs = []
    for g in range(16):
        sign = 1 if g % 2 == 0 else -1
        for y in range(16):
            target = (g + sign * step_x) % 16 * 16 + (y + sign * step_y) % 16
            pairs.append((g * 16 + y, target))
    return pairs


def body(state, register):
    axes = ("gx", "yz")
    shape = (5, 16, 16, 256)
    even = lax.rem(lax.axis_index("gx"), 2) == 0
    even_flag = jnp.reshape(even.astype(jnp.int32), (1,))
    lines = (16, 2, 5, 2, 128)

    y_send = pltpu.VMEM((5, 16, 4, 256), F32)
    x_send = pltpu.VMEM((5, 4, 16, 256), F32)
    state, ya, yb, xa, xb = pl.pallas_call(
        pack_kernel,
        out_shape=(pltpu.VMEM(shape, F32), y_send, y_send, x_send, x_send),
        in_specs=[SMEM, ANY],
        out_specs=(VMEM,) * 5,
        scratch_shapes=[pltpu.SemaphoreType.DMA((5,))],
        compiler_params=GRANT,
        name="pack",
    )(even_flag, state)
    ya = lax.ppermute(ya, axes, permutation(0, 1))
    yb = lax.ppermute(yb, axes, permutation(0, -1))
    xa = lax.ppermute(xa, axes, permutation(1, 0))
    xb = lax.ppermute(xb, axes, permutation(-1, 0))

    state = near(state)
    part = pl.pallas_call(
        inner_kernel,
        out_shape=pltpu.VMEM(shape, F32),
        in_specs=[VMEM],
        out_specs=VMEM,
        scratch_shapes=[pltpu.VMEM((6, 16, 16, 256), F32)],
        compiler_params=GRANT,
        name="inner",
    )(state)

    block = jax.ShapeDtypeStruct(shape, F32)
    send = pltpu.VMEM((5, 2, 16, 256), F32)
    register_out, section, moments, sa, sb = pl.pallas_call(
        edge_kernel,
        out_shape=(block, block, pltpu.VMEM(lines, F32), send, send),
        in_specs=[SMEM, VMEM, VMEM] + [ANY] * 5,
        out_specs=(ANY, ANY, VMEM, VMEM, VMEM),
        scratch_shapes=[
            pltpu.VMEM(shape, F32),
            pltpu.VMEM((2, 6, 4, 16, 256), F32),
            pltpu.VMEM((2, 6, 4, 16, 256), F32),
            pltpu.VMEM(shape, F32),
            pltpu.VMEM((5, 4, 16, 256), F32),
            pltpu.VMEM((5, 4, 16, 256), F32),
            pltpu.VMEM((5, 16, 4, 256), F32),
            pltpu.VMEM((5, 16, 4, 256), F32),
            pltpu.VMEM(shape, F32),
            pltpu.VMEM(shape, F32),
            pltpu.SemaphoreType.DMA((5,)),
            pltpu.SemaphoreType.DMA((2, 5)),
        ],
        compiler_params=GRANT,
        name="edge",
    )(even_flag, state, near(part), register, xa, xb, ya, yb)

    moments = lax.all_to_all(moments, "gx", 0, 0, tiled=True)
    sa = lax.ppermute(sa, axes, permutation(1, 0))
    sb = lax.ppermute(sb, axes, permutation(-1, 0))
    local = pl.pallas_call(
        local_kernel,
        out_shape=pltpu.VMEM(shape, F32),
        in_specs=[SMEM, ANY, VMEM, VMEM],
        out_specs=VMEM,
        scratch_shapes=[pltpu.VMEM(shape, F32), pltpu.SemaphoreType.DMA((5,))],
        compiler_params=GRANT,
        name="local",
    )(even_flag, section, sa, sb)
    sums = pl.pallas_call(
        ring_kernel,
        out_shape=pltpu.VMEM(lines, F32),
        in_specs=[VMEM, ANY],
        out_specs=VMEM,
        compiler_params=GRANT,
        name="ring",
    )(near(moments), local)
    sums = lax.all_to_all(sums, "gx", 0, 0, tiled=True)

    filtered = pl.pallas_call(
        filter_kernel,
        out_shape=jax.ShapeDtypeStruct(shape, F32),
        in_specs=[VMEM] * 2,
        out_specs=pl.BlockSpec(memory_space=pltpu.HBM),
        scratch_shapes=[
            pltpu.VMEM((2, 5, 16, 256), F32),
            pltpu.VMEM(shape, F32),
            pltpu.SemaphoreType.DMA((5,)),
        ],
        compiler_params=GRANT,
        name="filter",
    )(near(local), near(sums))
    return (register_out, filtered)


def solution(mesh):
    spec = P(None, "gx", "yz", None)
    return jax.shard_map(
        body, mesh=mesh, in_specs=(spec, spec), out_specs=(spec, spec), check_vma=False
    )
```

```python
import math

import jax
import jax.numpy as jnp
import numpy as np
from jax import lax
from jax.experimental import pallas as pl
from jax.experimental.pallas import tpu as pltpu
from jax.sharding import PartitionSpec as P


gamma_gas = 1.4
central_weights = (4.0 / 5.0, -1.0 / 5.0, 4.0 / 105.0, -1.0 / 280.0)
filter_alpha = 0.49
register_decay = -5.0 / 9.0
register_gain = 15.0 / 16.0
time_step = 0.2

ROOT = (-1.0 + math.sqrt(1.0 - 4.0 * filter_alpha**2)) / (2.0 * filter_alpha)
GREEN = 1.0 / math.sqrt(1.0 - 4.0 * filter_alpha**2)
TAPS = (
    (11.0 + 10.0 * filter_alpha) / 16.0,
    (15.0 + 34.0 * filter_alpha) / 64.0,
    (-3.0 + 6.0 * filter_alpha) / 32.0,
    (1.0 - 2.0 * filter_alpha) / 64.0,
)
KAPPA = GREEN * sum(TAPS[abs(n)] * ROOT**n for n in range(-3, 4))
DELTA = tuple(
    GREEN * sum(TAPS[abs(n)] * ROOT ** abs(d - n) for n in range(-3, 4)) - KAPPA * ROOT**d
    for d in range(3)
)

VMEM = pl.BlockSpec(memory_space=pltpu.VMEM)
SMEM = pl.BlockSpec(memory_space=pltpu.SMEM)
ANY = pl.BlockSpec(memory_space=pl.ANY)
F32 = jnp.float32
GRANT = pltpu.CompilerParams(vmem_limit_bytes=16 << 20)


def near(value):
    return pltpu.with_memory_space_constraint(value, pltpu.VMEM)


def primitives(fields):
    density, mom_x, mom_y, mom_z, energy = fields
    inverse = 1.0 / density
    speed_x, speed_y, speed_z = mom_x * inverse, mom_y * inverse, mom_z * inverse
    kinetic = 0.5 * (mom_x * speed_x + mom_y * speed_y + mom_z * speed_z)
    pressure = (gamma_gas - 1.0) * (energy - kinetic)
    return (density, speed_x, speed_y, speed_z, pressure, (energy + pressure) * inverse)


def pair_flux(left, right, direction, weight):
    density, speed_x, speed_y, speed_z, pressure, enthalpy = [a + b for a, b in zip(left, right)]
    normal = (speed_x, speed_y, speed_z)[direction]
    mass = (density * normal) * (0.25 * weight)
    moment = [mass * speed_x, mass * speed_y, mass * speed_z]
    moment[direction] = moment[direction] + pressure * weight
    return [mass + mass] + moment + [mass * enthalpy]


def rows_of(shape, dim):
    return lax.broadcasted_iota(jnp.int32, shape, dim)


def pack_kernel(even_ref, state_any, state_ref, ya_ref, yb_ref, xa_ref, xb_ref, sems):
    copies = [pltpu.make_async_copy(state_any.at[f], state_ref.at[f], sems.at[f]) for f in range(5)]
    for copy in copies:
        copy.start()
    even = even_ref[0] == 1
    for f in range(5):
        copies[f].wait()

        @pl.loop(0, 4)
        def _(step):
            for k in range(4):
                x = 4 * step + k
                low, high = state_ref[f, x, 0:4, :], state_ref[f, x, 12:16, :]
                ya_ref[f, x] = jnp.where(even, high, low)
                yb_ref[f, x] = jnp.where(even, low, high)
            xa_ref[f, step] = state_ref[f, jnp.where(even, 12, 0) + step]
            xb_ref[f, step] = state_ref[f, jnp.where(even, 0, 12) + step]


def difference_matrix():
    cell = np.arange(256)
    matrix = np.zeros((256, 256), np.float32)
    for l, weight in enumerate((672, -168, 32, -3), 1):
        matrix[(cell + l) % 256, cell] += weight
        matrix[(cell - l) % 256, cell] -= weight
    return jnp.asarray(np.concatenate([matrix, matrix]), jnp.bfloat16)


def inner_kernel(state_ref, matrix_ref, part_ref, prim_ref):
    row = rows_of((16, 128), 0)
    below = [jnp.where(row < 16 - l, F32(central_weights[l - 1]), F32(0.0)) for l in range(1, 5)]

    @pl.loop(0, 16)
    def _(x):
        state = [state_ref[f, x] for f in range(5)]
        prims = primitives(state)
        for f in range(6):
            prim_ref[f, x] = prims[f]
        density, speed_x, speed_y, speed_z, pressure, enthalpy = prims
        momentum = state[3]
        carried = (speed_x, speed_y, speed_z, enthalpy)
        dense = (state[1], state[2], state[3], state[4] + pressure)
        triple = [momentum * value for value in carried]
        triple[2] = triple[2] + 4.0 * pressure
        double = [speed_z * value for value in carried]
        fields = [density, *carried, *dense, *double, *triple]
        stack = jnp.concatenate(fields, axis=0)
        high = stack.astype(jnp.bfloat16)
        low = (stack - high.astype(F32)).astype(jnp.bfloat16)
        slopes = jnp.dot(
            jnp.concatenate([high, low], axis=1), matrix_ref[...], preferred_element_type=F32
        )
        slopes = [slopes[16 * k : 16 * k + 16] for k in range(17)]
        mass = slopes[7] + density * slopes[3] + speed_z * slopes[0]
        along = [(-1.0 / 1680.0) * mass]
        for k in range(4):
            value = slopes[13 + k] + density * slopes[9 + k] + speed_z * slopes[5 + k]
            value = value + momentum * slopes[1 + k] + carried[k] * mass
            along.append((-1.0 / 3360.0) * value)
        for half in range(2):
            lanes = pl.ds(128 * half, 128)
            cut = slice(128 * half, 128 * half + 128)
            own = [value[:, cut] for value in prims]
            total = [value[:, cut] for value in along]
            for l in range(1, 5):
                ahead = [pltpu.roll(value, 16 - l, 0) for value in own]
                flux = pair_flux(own, ahead, 1, below[l - 1])
                total = [part + (pltpu.roll(value, l, 0) - value) for part, value in zip(total, flux)]
            for f in range(5):
                part_ref[f, x, :, lanes] = total[f]

    for half in range(2):
        lanes = pl.ds(128 * half, 128)

        @pl.loop(0, 2)
        def _(tile):
            rows = pl.ds(pl.multiple_of(8 * tile, 8), 8)
            for x in range(16):
                own = [prim_ref[f, x, rows, lanes] for f in range(6)]
                total = [part_ref[f, x, rows, lanes] for f in range(5)]
                for l in range(1, min(5, 16 - x)):
                    ahead = [prim_ref[f, x + l, rows, lanes] for f in range(6)]
                    flux = pair_flux(own, ahead, 0, central_weights[l - 1])
                    for f in range(5):
                        total[f] = total[f] - flux[f]
                        part_ref[f, x + l, rows, lanes] = part_ref[f, x + l, rows, lanes] + flux[f]
                for f in range(5):
                    part_ref[f, x, rows, lanes] = total[f]


def edge_kernel(
    even_ref, state_ref, part_ref, register_ref, xa_ref, xb_ref, ya_ref, yb_ref,
    out_any, section_ref, moment_ref, sa_ref, sb_ref,
    acc_ref, prim_ref, far_ref, out_ref, out_sems,
):
    even = even_ref[0] == 1
    row = rows_of((8, 128), 0)
    departures = [pltpu.make_async_copy(out_ref.at[f], out_any.at[f], out_sems.at[f]) for f in range(5)]

    @pl.loop(4, 12)
    def _(x):
        for f in range(5):
            acc_ref[f, x] = part_ref[f, x]

    @pl.loop(0, 4)
    def _(x):
        for tile in range(2):
            rows = pl.ds(8 * tile, 8)
            first = primitives([state_ref[f, x, rows, :] for f in range(5)])
            last = primitives([state_ref[f, x + 12, rows, :] for f in range(5)])
            for f in range(6):
                prim_ref[0, f, x, rows, :] = first[f]
                prim_ref[1, f, x, rows, :] = last[f]

    @pl.loop(0, 4)
    def _(x):
        for tile in range(2):
            rows = pl.ds(8 * tile, 8)
            a = [xa_ref[f, x, rows, :] for f in range(5)]
            b = [xb_ref[f, x, rows, :] for f in range(5)]
            before = primitives([jnp.where(even, v, u) for u, v in zip(a, b)])
            after = primitives([jnp.where(even, u, v) for u, v in zip(a, b)])
            for f in range(6):
                far_ref[0, f, x, rows, :] = before[f]
                far_ref[1, f, x, rows, :] = after[f]

    for half in range(2):
        lanes = pl.ds(128 * half, 128)

        @pl.loop(0, 2)
        def _(tile):
            rows = pl.ds(pl.multiple_of(8 * tile, 8), 8)
            for x in range(4):
                own = [prim_ref[0, f, x, rows, lanes] for f in range(6)]
                total = [part_ref[f, x, rows, lanes] for f in range(5)]
                for l in range(x + 1, 5):
                    left = [far_ref[0, f, 4 + x - l, rows, lanes] for f in range(6)]
                    flux = pair_flux(left, own, 0, central_weights[l - 1])
                    total = [part + value for part, value in zip(total, flux)]
                for f in range(5):
                    acc_ref[f, x, rows, lanes] = total[f]
            for x in range(4):
                own = [prim_ref[1, f, x, rows, lanes] for f in range(6)]
                total = [part_ref[f, x + 12, rows, lanes] for f in range(5)]
                for l in range(4 - x, 5):
                    right = [far_ref[1, f, x + l - 4, rows, lanes] for f in range(6)]
                    flux = pair_flux(own, right, 0, central_weights[l - 1])
                    total = [part - value for part, value in zip(total, flux)]
                for f in range(5):
                    acc_ref[f, x + 12, rows, lanes] = total[f]

    @pl.loop(0, 16)
    def _(x):
        for half in range(2):
            lanes = pl.ds(128 * half, 128)
            left, right = [], []
            for f in range(5):
                a, b = ya_ref[f, x, :, lanes], yb_ref[f, x, :, lanes]
                below, above = jnp.where(even, a, b), jnp.where(even, b, a)
                left.append(jnp.concatenate([below, state_ref[f, x, 12:16, lanes]], axis=0))
                right.append(jnp.concatenate([state_ref[f, x, 0:4, lanes], above], axis=0))
            left, right = primitives(left), primitives(right)
            low = [jnp.zeros((8, 128), F32)] * 5
            high = [jnp.zeros((8, 128), F32)] * 5
            for l in range(1, 5):
                weight = jnp.where(lax.rem(row, 4) >= 4 - l, F32(central_weights[l - 1]), F32(0.0))
                other = right if l == 4 else [pltpu.roll(value, 4 - l, 0) for value in right]
                flux = pair_flux(left, other, 1, weight)
                high = [part - value for part, value in zip(high, flux)]
                back = flux if l == 4 else [pltpu.roll(value, 4 + l, 0) for value in flux]
                low = [part + value for part, value in zip(low, back)]
            for f in range(5):
                acc_ref[f, x, 0:8, lanes] = acc_ref[f, x, 0:8, lanes] + jnp.where(row < 4, low[f], 0.0)
                acc_ref[f, x, 8:16, lanes] = acc_ref[f, x, 8:16, lanes] + jnp.where(row >= 4, high[f], 0.0)

    for f in range(5):

        @pl.loop(0, 2)
        def _(tile):
            rows = pl.ds(pl.multiple_of(8 * tile, 8), 8)
            forward = jnp.zeros((8, 256), F32)
            backward = jnp.zeros((8, 256), F32)
            for x in range(16):
                value = register_decay * register_ref[f, x, rows, :] + time_step * acc_ref[f, x, rows, :]
                out_ref[f, x, rows, :] = value
                value = state_ref[f, x, rows, :] + register_gain * value
                section_ref[f, x, rows, :] = value
                forward = value + ROOT * forward
                backward = backward + ROOT**x * value
            for pair in range(4):
                for half in range(2):
                    q = 2 * (4 * tile + pair) + half
                    lanes = slice(128 * half, 128 * half + 128)
                    moment_ref[q, 0, f] = forward[2 * pair : 2 * pair + 2, lanes]
                    moment_ref[q, 1, f] = backward[2 * pair : 2 * pair + 2, lanes]

        departures[f].start()
        for k in range(2):
            sa_ref[f, k] = section_ref[f, jnp.where(even, 14, 0) + k]
            sb_ref[f, k] = section_ref[f, jnp.where(even, 0, 14) + k]
    for copy in departures:
        copy.wait()


def ring_kernel(moment_ref, local_any, sums_ref):
    decay = ROOT**16
    close = 1.0 / (1.0 - ROOT**256)
    for f in range(5):
        value = jnp.zeros((2, 128), F32)
        for p in range(16):
            value = moment_ref[p, 0, f] + decay * value
        value = value * close
        for p in range(16):
            sums_ref[p, 0, f] = value
            value = moment_ref[p, 0, f] + decay * value
        value = jnp.zeros((2, 128), F32)
        for p in reversed(range(16)):
            value = moment_ref[p, 1, f] + decay * value
        value = value * close
        for p in reversed(range(16)):
            sums_ref[p, 1, f] = value
            value = moment_ref[p, 1, f] + decay * value


def local_kernel(even_ref, section_ref, xa_ref, xb_ref, out_ref):
    even = even_ref[0] == 1
    for f in range(5):

        @pl.loop(0, 2)
        def _(tile):
            for half in range(2):
                rows, lanes = pl.ds(pl.multiple_of(8 * tile, 8), 8), pl.ds(128 * half, 128)
                a = [xa_ref[f, k, rows, lanes] for k in range(2)]
                b = [xb_ref[f, k, rows, lanes] for k in range(2)]
                cells = [jnp.where(even, v, u) for u, v in zip(a, b)]
                cells += [section_ref[f, x, rows, lanes] for x in range(16)]
                cells += [jnp.where(even, u, v) for u, v in zip(a, b)]
                value = cells[2]
                forward = [value]
                for x in range(1, 16):
                    value = cells[x + 2] + ROOT * value
                    forward.append(value)
                value = jnp.zeros((8, 128), F32)
                for x in reversed(range(16)):
                    value = cells[x + 2] + ROOT * value
                    out_ref[f, x, rows, lanes] = (
                        KAPPA * (forward[x] + value)
                        + (DELTA[0] - KAPPA) * cells[x + 2]
                        + DELTA[1] * (cells[x + 1] + cells[x + 3])
                        + DELTA[2] * (cells[x] + cells[x + 4])
                    )


def filter_kernel(local_ref, sums_ref, out_ref, ends_ref, full_ref, sems):
    for q in range(16):
        rows = pl.ds(2 * (q // 2), 2)
        lanes = pl.ds(128 * (q % 2), 128)
        for f in range(5):
            ends_ref[0, f, rows, lanes] = sums_ref[q, 0, f]
            ends_ref[1, f, rows, lanes] = sums_ref[q, 1, f]
    copies = [pltpu.make_async_copy(full_ref.at[f], out_ref.at[f], sems.at[f]) for f in range(5)]
    for f in range(5):

        @pl.loop(0, 2)
        def _(tile):
            rows = pl.ds(pl.multiple_of(8 * tile, 8), 8)
            before, after = ends_ref[0, f, rows, :], ends_ref[1, f, rows, :]
            for x in range(16):
                full_ref[f, x, rows, :] = local_ref[f, x, rows, :] + (
                    KAPPA * ROOT ** (x + 1) * before + KAPPA * ROOT ** (16 - x) * after
                )

        copies[f].start()
    for copy in copies:
        copy.wait()


def permutation(step_x, step_y):
    pairs = []
    for g in range(16):
        sign = 1 if g % 2 == 0 else -1
        for y in range(16):
            target = (g + sign * step_x) % 16 * 16 + (y + sign * step_y) % 16
            pairs.append((g * 16 + y, target))
    return pairs


def body(state, register):
    axes = ("gx", "yz")
    shape = (5, 16, 16, 256)
    even = lax.rem(lax.axis_index("gx"), 2) == 0
    even_flag = jnp.reshape(even.astype(jnp.int32), (1,))
    lines = (16, 2, 5, 2, 128)

    y_send = pltpu.VMEM((5, 16, 4, 256), F32)
    x_send = pltpu.VMEM((5, 4, 16, 256), F32)
    state, ya, yb, xa, xb = pl.pallas_call(
        pack_kernel,
        out_shape=(pltpu.VMEM(shape, F32), y_send, y_send, x_send, x_send),
        in_specs=[SMEM, ANY],
        out_specs=(VMEM,) * 5,
        scratch_shapes=[pltpu.SemaphoreType.DMA((5,))],
        compiler_params=GRANT,
        name="pack",
    )(even_flag, pltpu.with_memory_space_constraint(state, pltpu.HBM))
    ya = lax.ppermute(ya, axes, permutation(0, 1))
    yb = lax.ppermute(yb, axes, permutation(0, -1))
    xa = lax.ppermute(xa, axes, permutation(1, 0))
    xb = lax.ppermute(xb, axes, permutation(-1, 0))

    state = near(state)
    part = pl.pallas_call(
        inner_kernel,
        out_shape=pltpu.VMEM(shape, F32),
        in_specs=[VMEM, VMEM],
        out_specs=VMEM,
        scratch_shapes=[pltpu.VMEM((6, 16, 16, 256), F32)],
        compiler_params=GRANT,
        name="inner",
    )(state, near(difference_matrix()))

    block = jax.ShapeDtypeStruct(shape, F32)
    send = pltpu.VMEM((5, 2, 16, 256), F32)
    register_out, section, moments, sa, sb = pl.pallas_call(
        edge_kernel,
        out_shape=(block, pltpu.VMEM(shape, F32), pltpu.VMEM(lines, F32), send, send),
        in_specs=[SMEM] + [VMEM] * 7,
        out_specs=(pl.BlockSpec(memory_space=pltpu.HBM),) + (VMEM,) * 4,
        scratch_shapes=[
            pltpu.VMEM(shape, F32),
            pltpu.VMEM((2, 6, 4, 16, 256), F32),
            pltpu.VMEM((2, 6, 4, 16, 256), F32),
            pltpu.VMEM(shape, F32),
            pltpu.SemaphoreType.DMA((5,)),
        ],
        compiler_params=GRANT,
        name="edge",
    )(even_flag, state, near(part), near(register), near(xa), near(xb), near(ya), near(yb))

    moments = lax.all_to_all(moments, "gx", 0, 0, tiled=True)
    sa = lax.ppermute(sa, axes, permutation(1, 0))
    sb = lax.ppermute(sb, axes, permutation(-1, 0))
    local = pl.pallas_call(
        local_kernel,
        out_shape=pltpu.VMEM(shape, F32),
        in_specs=[SMEM] + [VMEM] * 3,
        out_specs=VMEM,
        compiler_params=GRANT,
        name="local",
    )(even_flag, near(section), near(sa), near(sb))
    sums = pl.pallas_call(
        ring_kernel,
        out_shape=pltpu.VMEM(lines, F32),
        in_specs=[VMEM, ANY],
        out_specs=VMEM,
        compiler_params=GRANT,
        name="ring",
    )(near(moments), local)
    sums = lax.all_to_all(sums, "gx", 0, 0, tiled=True)

    filtered = pl.pallas_call(
        filter_kernel,
        out_shape=jax.ShapeDtypeStruct(shape, F32),
        in_specs=[VMEM] * 2,
        out_specs=pl.BlockSpec(memory_space=pltpu.HBM),
        scratch_shapes=[
            pltpu.VMEM((2, 5, 16, 256), F32),
            pltpu.VMEM(shape, F32),
            pltpu.SemaphoreType.DMA((5,)),
        ],
        compiler_params=GRANT,
        name="filter",
    )(near(local), near(sums))
    return (register_out, filtered)


def solution(mesh):
    spec = P(None, "gx", "yz", None)
    return jax.shard_map(body, mesh=mesh, in_specs=(spec, spec), out_specs=(spec, spec), check_vma=False)
```

```python
import math

import jax
import jax.numpy as jnp
import numpy as np
from jax import lax
from jax.experimental import pallas as pl
from jax.experimental.pallas import tpu as pltpu
from jax.sharding import PartitionSpec as P


gamma_gas = 1.4
central_weights = (4.0 / 5.0, -1.0 / 5.0, 4.0 / 105.0, -1.0 / 280.0)
filter_alpha = 0.49
register_decay = -5.0 / 9.0
register_gain = 15.0 / 16.0
time_step = 0.2

ROOT = (-1.0 + math.sqrt(1.0 - 4.0 * filter_alpha**2)) / (2.0 * filter_alpha)
GREEN = 1.0 / math.sqrt(1.0 - 4.0 * filter_alpha**2)
TAPS = (
    (11.0 + 10.0 * filter_alpha) / 16.0,
    (15.0 + 34.0 * filter_alpha) / 64.0,
    (-3.0 + 6.0 * filter_alpha) / 32.0,
    (1.0 - 2.0 * filter_alpha) / 64.0,
)
KAPPA = GREEN * sum(TAPS[abs(n)] * ROOT**n for n in range(-3, 4))
DELTA = tuple(
    GREEN * sum(TAPS[abs(n)] * ROOT ** abs(d - n) for n in range(-3, 4)) - KAPPA * ROOT**d
    for d in range(3)
)

VMEM = pl.BlockSpec(memory_space=pltpu.VMEM)
SMEM = pl.BlockSpec(memory_space=pltpu.SMEM)
ANY = pl.BlockSpec(memory_space=pl.ANY)
F32 = jnp.float32
SHARE = register_gain * time_step
GRANT = pltpu.CompilerParams(vmem_limit_bytes=16 << 20)


def near(value):
    return pltpu.with_memory_space_constraint(value, pltpu.VMEM)


def far(value):
    return pltpu.with_memory_space_constraint(value, pltpu.HBM)


def primitives(fields):
    density, mom_x, mom_y, mom_z, energy = fields
    inverse = 1.0 / density
    speed_x, speed_y, speed_z = mom_x * inverse, mom_y * inverse, mom_z * inverse
    kinetic = 0.5 * (mom_x * speed_x + mom_y * speed_y + mom_z * speed_z)
    pressure = (gamma_gas - 1.0) * (energy - kinetic)
    return (density, speed_x, speed_y, speed_z, pressure, (energy + pressure) * inverse)


def pair_flux(left, right, direction, weight):
    density, speed_x, speed_y, speed_z, pressure, enthalpy = [a + b for a, b in zip(left, right)]
    normal = (speed_x, speed_y, speed_z)[direction]
    mass = (density * normal) * (0.25 * weight)
    moment = [mass * speed_x, mass * speed_y, mass * speed_z]
    moment[direction] = moment[direction] + pressure * weight
    return [mass + mass] + moment + [mass * enthalpy]


def rows_of(shape, dim):
    return lax.broadcasted_iota(jnp.int32, shape, dim)


def pack_kernel(even_ref, state_any, state_ref, ya_ref, yb_ref, xa_ref, xb_ref, sems):
    copies = [pltpu.make_async_copy(state_any.at[f], state_ref.at[f], sems.at[f]) for f in range(5)]
    for copy in copies:
        copy.start()
    even = even_ref[0] == 1
    for f in range(5):
        copies[f].wait()

        @pl.loop(0, 4)
        def _(step):
            for k in range(4):
                x = 4 * step + k
                low, high = state_ref[f, x, 0:4, :], state_ref[f, x, 12:16, :]
                ya_ref[f, x] = jnp.where(even, high, low)
                yb_ref[f, x] = jnp.where(even, low, high)
            xa_ref[f, step] = state_ref[f, jnp.where(even, 12, 0) + step]
            xb_ref[f, step] = state_ref[f, jnp.where(even, 0, 12) + step]


def difference_matrix():
    cell = np.arange(256)
    matrix = np.zeros((256, 256), np.float32)
    for l, weight in enumerate((672, -168, 32, -3), 1):
        matrix[(cell + l) % 256, cell] += weight
        matrix[(cell - l) % 256, cell] -= weight
    return jnp.asarray(np.concatenate([matrix, matrix]), jnp.bfloat16)


def inner_kernel(state_ref, matrix_ref, part_ref, prim_ref):
    row = rows_of((16, 128), 0)
    below = [jnp.where(row < 16 - l, F32(central_weights[l - 1]), F32(0.0)) for l in range(1, 5)]

    @pl.loop(0, 16)
    def _(x):
        state = [state_ref[f, x] for f in range(5)]
        prims = primitives(state)
        for f in range(6):
            prim_ref[f, x] = prims[f]
        density, speed_x, speed_y, speed_z, pressure, enthalpy = prims
        momentum = state[3]
        carried = (speed_x, speed_y, speed_z, enthalpy)
        dense = (state[1], state[2], state[3], state[4] + pressure)
        triple = [momentum * value for value in carried]
        triple[2] = triple[2] + 4.0 * pressure
        double = [speed_z * value for value in carried]
        fields = [density, *carried, *dense, *double, *triple]
        stack = jnp.concatenate(fields, axis=0)
        high = stack.astype(jnp.bfloat16)
        low = (stack - high.astype(F32)).astype(jnp.bfloat16)
        slopes = jnp.dot(
            jnp.concatenate([high, low], axis=1), matrix_ref[...], preferred_element_type=F32
        )
        slopes = [slopes[16 * k : 16 * k + 16] for k in range(17)]
        mass = slopes[7] + density * slopes[3] + speed_z * slopes[0]
        along = [(-1.0 / 1680.0) * mass]
        for k in range(4):
            value = slopes[13 + k] + density * slopes[9 + k] + speed_z * slopes[5 + k]
            value = value + momentum * slopes[1 + k] + carried[k] * mass
            along.append((-1.0 / 3360.0) * value)
        for half in range(2):
            lanes = pl.ds(128 * half, 128)
            cut = slice(128 * half, 128 * half + 128)
            own = [value[:, cut] for value in prims]
            total = [value[:, cut] for value in along]
            for l in range(1, 5):
                ahead = [pltpu.roll(value, 16 - l, 0) for value in own]
                flux = pair_flux(own, ahead, 1, below[l - 1])
                total = [part + (pltpu.roll(value, l, 0) - value) for part, value in zip(total, flux)]
            for f in range(5):
                part_ref[f, x, :, lanes] = total[f]

    for half in range(2):
        lanes = pl.ds(128 * half, 128)

        @pl.loop(0, 2)
        def _(tile):
            rows = pl.ds(pl.multiple_of(8 * tile, 8), 8)
            for x in range(16):
                own = [prim_ref[f, x, rows, lanes] for f in range(6)]
                total = [part_ref[f, x, rows, lanes] for f in range(5)]
                for l in range(1, min(5, 16 - x)):
                    ahead = [prim_ref[f, x + l, rows, lanes] for f in range(6)]
                    flux = pair_flux(own, ahead, 0, central_weights[l - 1])
                    for f in range(5):
                        total[f] = total[f] - flux[f]
                        part_ref[f, x + l, rows, lanes] = part_ref[f, x + l, rows, lanes] + flux[f]
                for f in range(5):
                    part_ref[f, x, rows, lanes] = total[f]


def layer_kernel(
    even_ref, state_ref, part_ref, register_ref, xa_ref, xb_ref,
    base_ref, section_ref, sum_ref, acc_ref, prim_ref, far_ref,
):
    even = even_ref[0] == 1

    @pl.loop(0, 4)
    def _(x):
        for tile in range(2):
            rows = pl.ds(8 * tile, 8)
            first = primitives([state_ref[f, x, rows, :] for f in range(5)])
            last = primitives([state_ref[f, x + 12, rows, :] for f in range(5)])
            for f in range(6):
                prim_ref[0, f, x, rows, :] = first[f]
                prim_ref[1, f, x, rows, :] = last[f]

    @pl.loop(0, 4)
    def _(x):
        for tile in range(2):
            rows = pl.ds(8 * tile, 8)
            a = [xa_ref[f, x, rows, :] for f in range(5)]
            b = [xb_ref[f, x, rows, :] for f in range(5)]
            before = primitives([jnp.where(even, v, u) for u, v in zip(a, b)])
            after = primitives([jnp.where(even, u, v) for u, v in zip(a, b)])
            for f in range(6):
                far_ref[0, f, x, rows, :] = before[f]
                far_ref[1, f, x, rows, :] = after[f]

    for half in range(2):
        lanes = pl.ds(128 * half, 128)

        @pl.loop(0, 2)
        def _(tile):
            rows = pl.ds(pl.multiple_of(8 * tile, 8), 8)
            for x in range(4):
                own = [prim_ref[0, f, x, rows, lanes] for f in range(6)]
                total = [part_ref[f, x, rows, lanes] for f in range(5)]
                for l in range(x + 1, 5):
                    left = [far_ref[0, f, 4 + x - l, rows, lanes] for f in range(6)]
                    flux = pair_flux(left, own, 0, central_weights[l - 1])
                    total = [part + value for part, value in zip(total, flux)]
                for f in range(5):
                    acc_ref[f, x, rows, lanes] = total[f]
            for x in range(4):
                own = [prim_ref[1, f, x, rows, lanes] for f in range(6)]
                total = [part_ref[f, x + 12, rows, lanes] for f in range(5)]
                for l in range(4 - x, 5):
                    right = [far_ref[1, f, x + l - 4, rows, lanes] for f in range(6)]
                    flux = pair_flux(own, right, 0, central_weights[l - 1])
                    total = [part - value for part, value in zip(total, flux)]
                for f in range(5):
                    acc_ref[f, x + 12, rows, lanes] = total[f]

    for f in range(5):

        @pl.loop(0, 2)
        def _(tile):
            rows = pl.ds(pl.multiple_of(8 * tile, 8), 8)
            forward = jnp.zeros((8, 256), F32)
            backward = jnp.zeros((8, 256), F32)
            for x in range(16):
                source = part_ref if 4 <= x < 12 else acc_ref
                value = register_decay * register_ref[f, x, rows, :] + time_step * source[f, x, rows, :]
                base_ref[f, x, rows, :] = value
                value = state_ref[f, x, rows, :] + register_gain * value
                section_ref[f, x, rows, :] = value
                forward = value + ROOT * forward
                backward = backward + ROOT**x * value
            sum_ref[0, f, rows, :] = forward
            sum_ref[1, f, rows, :] = backward


def face_kernel(
    even_ref, state_ref, section_ref, sum_ref, ya_ref, yb_ref,
    delta_ref, moment_ref, sa_ref, sb_ref,
):
    even = even_ref[0] == 1
    row = rows_of((8, 128), 0)

    @pl.loop(0, 16)
    def _(x):
        for half in range(2):
            lanes = pl.ds(128 * half, 128)
            left, right = [], []
            for f in range(5):
                a, b = ya_ref[f, x, :, lanes], yb_ref[f, x, :, lanes]
                below, above = jnp.where(even, a, b), jnp.where(even, b, a)
                left.append(jnp.concatenate([below, state_ref[f, x, 12:16, lanes]], axis=0))
                right.append(jnp.concatenate([state_ref[f, x, 0:4, lanes], above], axis=0))
            left, right = primitives(left), primitives(right)
            low = [jnp.zeros((8, 128), F32)] * 5
            high = [jnp.zeros((8, 128), F32)] * 5
            for l in range(1, 5):
                weight = jnp.where(lax.rem(row, 4) >= 4 - l, F32(central_weights[l - 1]), F32(0.0))
                other = right if l == 4 else [pltpu.roll(value, 4 - l, 0) for value in right]
                flux = pair_flux(left, other, 1, weight)
                high = [part - value for part, value in zip(high, flux)]
                back = flux if l == 4 else [pltpu.roll(value, 4 + l, 0) for value in flux]
                low = [part + value for part, value in zip(low, back)]
            for f in range(5):
                delta_ref[f, x, :, lanes] = jnp.where(row < 4, low[f], high[f])

    wide = rows_of((8, 256), 0)
    for f in range(5):
        forward = jnp.zeros((8, 256), F32)
        backward = jnp.zeros((8, 256), F32)
        for x in range(16):
            value = delta_ref[f, x]
            forward = value + ROOT * forward
            backward = backward + ROOT**x * value
        for k, value in enumerate((forward, backward)):
            for tile in range(2):
                touched = wide < 4 if tile == 0 else wide >= 4
                value_here = sum_ref[k, f, 8 * tile : 8 * tile + 8, :] + jnp.where(touched, SHARE * value, 0.0)
                for pair in range(4):
                    for half in range(2):
                        q = 2 * (4 * tile + pair) + half
                        lanes = slice(128 * half, 128 * half + 128)
                        moment_ref[q, k, f] = value_here[2 * pair : 2 * pair + 2, lanes]
        for k in range(2):
            for target, x in ((sa_ref, jnp.where(even, 14, 0) + k), (sb_ref, jnp.where(even, 0, 14) + k)):
                for tile in range(2):
                    touched = wide < 4 if tile == 0 else wide >= 4
                    rows = slice(8 * tile, 8 * tile + 8)
                    target[f, k, rows, :] = section_ref[f, x, rows, :] + jnp.where(
                        touched, SHARE * delta_ref[f, x], 0.0
                    )


def ring_kernel(moment_ref, local_any, sa_any, sb_any, sums_ref):
    decay = ROOT**16
    close = 1.0 / (1.0 - ROOT**256)
    for f in range(5):
        value = jnp.zeros((2, 128), F32)
        for p in range(16):
            value = moment_ref[p, 0, f] + decay * value
        value = value * close
        for p in range(16):
            sums_ref[p, 0, f] = value
            value = moment_ref[p, 0, f] + decay * value
        value = jnp.zeros((2, 128), F32)
        for p in reversed(range(16)):
            value = moment_ref[p, 1, f] + decay * value
        value = value * close
        for p in reversed(range(16)):
            sums_ref[p, 1, f] = value
            value = moment_ref[p, 1, f] + decay * value


def local_kernel(
    section_any, delta_ref, base_any, out_ref, register_any, section_ref, base_ref, in_sems, out_sems
):
    sources = ((section_any, section_ref), (base_any, base_ref))
    arrivals = [
        [pltpu.make_async_copy(a.at[f], b.at[f], in_sems.at[k, f]) for k, (a, b) in enumerate(sources)] for f in range(5)
    ]
    departures = [pltpu.make_async_copy(base_ref.at[f], register_any.at[f], out_sems.at[f]) for f in range(5)]
    for group in arrivals:
        for copy in group:
            copy.start()
    row = rows_of((8, 128), 0)
    for f in range(5):
        for copy in arrivals[f]:
            copy.wait()
        for tile in range(2):
            rows = pl.ds(8 * tile, 8)
            touched = row < 4 if tile == 0 else row >= 4

            @pl.loop(0, 2)
            def _(half):
                lanes = pl.ds(pl.multiple_of(128 * half, 128), 128)
                cells = [None, None]
                for x in range(16):
                    change = jnp.where(touched, delta_ref[f, x, :, lanes], 0.0)
                    base_ref[f, x, rows, lanes] = base_ref[f, x, rows, lanes] + time_step * change
                    cells.append(section_ref[f, x, rows, lanes] + SHARE * change)
                cells += [None, None]
                value = cells[2]
                forward = [value]
                for x in range(1, 16):
                    value = cells[x + 2] + ROOT * value
                    forward.append(value)
                value = None
                for x in reversed(range(16)):
                    value = cells[x + 2] if value is None else cells[x + 2] + ROOT * value
                    result = KAPPA * (forward[x] + value) + (DELTA[0] - KAPPA) * cells[x + 2]
                    for d in (1, 2):
                        for other in (cells[x + 2 - d], cells[x + 2 + d]):
                            if other is not None:
                                result = result + DELTA[d] * other
                    out_ref[f, x, rows, lanes] = result

        departures[f].start()
    for copy in departures:
        copy.wait()


def filter_kernel(even_ref, local_ref, sums_ref, xa_ref, xb_ref, out_ref, ends_ref, full_ref, sems):
    even = even_ref[0] == 1
    for q in range(16):
        rows = pl.ds(2 * (q // 2), 2)
        lanes = pl.ds(128 * (q % 2), 128)
        for f in range(5):
            ends_ref[0, f, rows, lanes] = sums_ref[q, 0, f]
            ends_ref[1, f, rows, lanes] = sums_ref[q, 1, f]
    copies = [pltpu.make_async_copy(full_ref.at[f], out_ref.at[f], sems.at[f]) for f in range(5)]
    for f in range(5):

        @pl.loop(0, 2)
        def _(tile):
            rows = pl.ds(pl.multiple_of(8 * tile, 8), 8)
            before, after = ends_ref[0, f, rows, :], ends_ref[1, f, rows, :]
            a = [xa_ref[f, k, rows, :] for k in range(2)]
            b = [xb_ref[f, k, rows, :] for k in range(2)]
            left = [jnp.where(even, v, u) for u, v in zip(a, b)]
            right = [jnp.where(even, u, v) for u, v in zip(a, b)]
            near_ends = {
                0: DELTA[1] * left[1] + DELTA[2] * left[0],
                1: DELTA[2] * left[1],
                14: DELTA[2] * right[0],
                15: DELTA[1] * right[0] + DELTA[2] * right[1],
            }
            for x in range(16):
                value = local_ref[f, x, rows, :] + (
                    KAPPA * ROOT ** (x + 1) * before + KAPPA * ROOT ** (16 - x) * after
                )
                full_ref[f, x, rows, :] = value + near_ends[x] if x in near_ends else value

        copies[f].start()
    for copy in copies:
        copy.wait()


def permutation(step_x, step_y):
    pairs = []
    for g in range(16):
        sign = 1 if g % 2 == 0 else -1
        for y in range(16):
            target = (g + sign * step_x) % 16 * 16 + (y + sign * step_y) % 16
            pairs.append((g * 16 + y, target))
    return pairs


def body(state, register):
    axes = ("gx", "yz")
    shape = (5, 16, 16, 256)
    even = lax.rem(lax.axis_index("gx"), 2) == 0
    even_flag = jnp.reshape(even.astype(jnp.int32), (1,))
    lines = (16, 2, 5, 2, 128)

    y_send = pltpu.VMEM((5, 16, 4, 256), F32)
    x_send = pltpu.VMEM((5, 4, 16, 256), F32)
    state, ya, yb, xa, xb = pl.pallas_call(
        pack_kernel,
        out_shape=(pltpu.VMEM(shape, F32), y_send, y_send, x_send, x_send),
        in_specs=[SMEM, ANY],
        out_specs=(VMEM,) * 5,
        scratch_shapes=[pltpu.SemaphoreType.DMA((5,))],
        compiler_params=GRANT,
        name="pack",
    )(even_flag, far(state))
    ya = lax.ppermute(ya, axes, permutation(0, 1))
    yb = lax.ppermute(yb, axes, permutation(0, -1))
    xa = lax.ppermute(xa, axes, permutation(1, 0))
    xb = lax.ppermute(xb, axes, permutation(-1, 0))

    state = near(state)
    part = pl.pallas_call(
        inner_kernel,
        out_shape=pltpu.VMEM(shape, F32),
        in_specs=[VMEM, VMEM],
        out_specs=VMEM,
        scratch_shapes=[pltpu.VMEM((6, 16, 16, 256), F32)],
        compiler_params=GRANT,
        name="inner",
    )(state, near(difference_matrix()))

    block = jax.ShapeDtypeStruct(shape, F32)
    send = pltpu.VMEM((5, 2, 16, 256), F32)
    hbm = pl.BlockSpec(memory_space=pltpu.HBM)
    base, section, block_sums = pl.pallas_call(
        layer_kernel,
        out_shape=(pltpu.VMEM(shape, F32), pltpu.VMEM(shape, F32), pltpu.VMEM((2, 5, 16, 256), F32)),
        in_specs=[SMEM] + [VMEM] * 5,
        out_specs=(VMEM, VMEM, VMEM),
        scratch_shapes=[
            pltpu.VMEM(shape, F32),
            pltpu.VMEM((2, 6, 4, 16, 256), F32),
            pltpu.VMEM((2, 6, 4, 16, 256), F32),
        ],
        compiler_params=GRANT,
        name="layer",
    )(even_flag, state, near(part), near(register), near(xa), near(xb))

    delta, moments, sa, sb = pl.pallas_call(
        face_kernel,
        out_shape=(pltpu.VMEM((5, 16, 8, 256), F32), pltpu.VMEM(lines, F32), send, send),
        in_specs=[SMEM] + [VMEM] * 5,
        out_specs=(VMEM,) * 4,
        compiler_params=GRANT,
        name="face",
    )(even_flag, state, near(section), near(block_sums), near(ya), near(yb))

    moments = lax.all_to_all(moments, "gx", 0, 0, tiled=True)
    sa = lax.ppermute(sa, axes, permutation(1, 0))
    sb = lax.ppermute(sb, axes, permutation(-1, 0))
    local, register_out = pl.pallas_call(
        local_kernel,
        out_shape=(pltpu.VMEM(shape, F32), block),
        in_specs=[ANY, VMEM, ANY],
        out_specs=(VMEM, hbm),
        scratch_shapes=[
            pltpu.VMEM(shape, F32),
            pltpu.VMEM(shape, F32),
            pltpu.SemaphoreType.DMA((2, 5)),
            pltpu.SemaphoreType.DMA((5,)),
        ],
        compiler_params=GRANT,
        name="local",
    )(far(section), near(delta), far(base))
    sums = pl.pallas_call(
        ring_kernel,
        out_shape=pltpu.VMEM(lines, F32),
        in_specs=[VMEM, ANY, ANY, ANY],
        out_specs=VMEM,
        compiler_params=GRANT,
        name="ring",
    )(near(moments), local, sa, sb)
    sums = lax.all_to_all(sums, "gx", 0, 0, tiled=True)

    filtered = pl.pallas_call(
        filter_kernel,
        out_shape=jax.ShapeDtypeStruct(shape, F32),
        in_specs=[SMEM] + [VMEM] * 4,
        out_specs=hbm,
        scratch_shapes=[
            pltpu.VMEM((2, 5, 16, 256), F32),
            pltpu.VMEM(shape, F32),
            pltpu.SemaphoreType.DMA((5,)),
        ],
        compiler_params=GRANT,
        name="filter",
    )(even_flag, near(local), near(sums), near(sa), near(sb))
    return (register_out, filtered)


def solution(mesh):
    spec = P(None, "gx", "yz", None)
    return jax.shard_map(body, mesh=mesh, in_specs=(spec, spec), out_specs=(spec, spec), check_vma=False)
```
